32 devices in a mesh: kf: 8 (over z, y), kc: 4 (over x, core).
Axes of the slice: x: 2, y: 2, z: 4, core: 2. Of those that a mesh axis runs over, the one named last changes fastest.
Arguments:
- kernel_coarse: bfloat16 [256, 256], P('kf'), may hold values from -6 to 6
- coefficients: bfloat16 [128, 256], P(('kf', 'kc')), may hold values from -1.5 to 1.5
- nearest: int32 [128], replicated, may hold values from 0 to 15
Outputs:
- kernel_fine: bfloat16 [2048, 2048], P('kf', 'kc')
The draws below stay inside these ranges and needn't reach their ends.
All inputs are finite; a program needn't handle non-finite values.
Results may differ from the reference program's by a relative error of at most 0.0049.
Values may be sent and summed in bfloat16 or wider, within the bound.
A program may use at most 64 MiB of HBM per device.

```python
import jax
import jax.numpy as jnp
from jax import lax

P_SIZE = 16
FK_DEV = 16
FINE = 128
COARSE = 16
N_KF = 8


def touch_ends(entries, stream_key, low, largest):
    index_at = [jax.random.randint(jax.random.fold_in(stream_key, axis), (), 0, length) for axis, length in enumerate(entries.shape)]
    widest = entries.shape.index(max(entries.shape))
    neighbour = index_at[:widest] + [(index_at[widest] + 1) % entries.shape[widest]] + index_at[widest + 1:]
    return entries.at[tuple(index_at)].set(low).at[tuple(neighbour)].set(largest)


def steps_of(own_key, shape, cuts, least, top_value):
    loudness, own = 1.0, jax.random.fold_in(own_key, 6)
    for position, blocks in cuts:
        draws = jnp.exp(jax.random.uniform(jax.random.fold_in(own, position), (blocks,), jnp.float32, least / len(cuts), top_value / len(cuts)))
        loudness = loudness * jnp.repeat(draws, shape[position] // blocks).reshape([-1 if axis == position else 1 for axis in range(len(shape))])
    return loudness


def gaussian(stream_key, shape, spread, reach, shards=(), kind=jnp.bfloat16):
    array = spread * jax.random.normal(stream_key, shape, jnp.float32)
    if shards:
        array = array * steps_of(stream_key, shape, shards, -0.22, 0.18)
    return jnp.clip(array, -reach, reach).astype(kind)


def setup_inputs(seed: int = 0) -> dict:
    streams_of = jax.random.split(jax.random.key(seed), 4)
    return {
        "kernel_coarse": gaussian(streams_of[0], (COARSE * P_SIZE, COARSE * P_SIZE), 1.0, 6.0, ((0, 8),)),
        "coefficients": gaussian(streams_of[1], (FINE, P_SIZE * P_SIZE), P_SIZE ** -0.5, 1.5, ((0, 32),)),
        "nearest": touch_ends(jax.random.randint(streams_of[2], (FINE,), 0, COARSE), jax.random.fold_in(streams_of[2], 1), 0, COARSE - 1).astype(jnp.int32),
    }


def reference(kernel_coarse, coefficients, nearest):
    offsets = jnp.arange(P_SIZE, dtype=jnp.int32)
    columns = (nearest[:, None] * P_SIZE + offsets[None, :]).reshape(-1)
    coef_all = coefficients.reshape(FINE, P_SIZE, P_SIZE).astype(jnp.float32)
    gathered = jnp.take(kernel_coarse, columns, axis=1).astype(jnp.float32).reshape(COARSE * P_SIZE, FINE, P_SIZE)
    rotated = jnp.einsum("ckn,kan->cka", gathered, coef_all).astype(jnp.bfloat16).reshape(COARSE, P_SIZE, FINE * P_SIZE)

    def expand(block_index):
        col_points = lax.dynamic_slice_in_dim(nearest, block_index * FK_DEV, FK_DEV)
        coef_block = lax.dynamic_slice_in_dim(coef_all, block_index * FK_DEV, FK_DEV, 0)
        picked = jnp.take(rotated, col_points, axis=0).astype(jnp.float32)
        return jnp.einsum("jnr,jbn->jbr", picked, coef_block).astype(jnp.bfloat16)

    blocks = lax.map(expand, jnp.arange(N_KF, dtype=jnp.int32))
    return blocks.reshape(FINE * P_SIZE, FINE * P_SIZE).T
```

```python
import functools
import math

import jax
import jax.numpy as jnp
from jax import lax
from jax.experimental import pallas as pl
from jax.experimental.pallas import tpu as pltpu
from jax.sharding import PartitionSpec as P

UNROLL_LIMIT = 16
CHUNK_SLOTS = 8


def each(low, high, step):
    if high - low <= UNROLL_LIMIT:
        for index in range(low, high):
            step(index)
    else:
        lax.fori_loop(low, high, lambda index, carry: (step(index), carry)[1], 0)


def remote(source, target, send_sem, recv_sem, kf, kc):
    return pltpu.make_async_remote_copy(
        src_ref=source,
        dst_ref=target,
        send_sem=send_sem,
        recv_sem=recv_sem,
        device_id={"kf": kf, "kc": kc},
        device_id_type=pl.DeviceIdType.MESH,
    )


def signal(barrier, kf, kc):
    pl.semaphore_signal(
        barrier, inc=1, device_id={"kf": kf, "kc": kc}, device_id_type=pl.DeviceIdType.MESH
    )


def expand(blocks, near, first_point, spread, target):
    slot_count, points, width = blocks.shape
    pairs = math.isqrt(width)
    column_total = target.shape[1]
    chunk = min(slot_count, CHUNK_SLOTS)
    own_block = (
        lax.broadcasted_iota(jnp.int32, (pairs, width), 1) // pairs
        == lax.broadcasted_iota(jnp.int32, (pairs, width), 0)
    )
    coarse_of = lax.broadcasted_iota(jnp.int32, (pairs, column_total), 1) // pairs
    fold = (
        lax.broadcasted_iota(jnp.int32, (width, column_total), 0) % pairs
        == lax.broadcasted_iota(jnp.int32, (width, column_total), 1) % pairs
    ).astype(jnp.bfloat16)
    chunk_points = chunk * points

    def step(part):
        for slot in range(chunk):
            block = blocks[part * chunk + slot].astype(jnp.float32)
            for point in range(points):
                row = jnp.broadcast_to(block[point : point + 1, :], (pairs, width))
                place = (slot * points + point) * pairs
                spread[place : place + pairs, :] = jnp.where(own_block, row, 0.0).astype(jnp.bfloat16)
        tiled = jnp.dot(
            spread[: chunk_points * pairs, :], fold, preferred_element_type=jnp.float32
        )
        for point in range(chunk_points):
            place = point * pairs
            wanted = near[first_point + part * chunk_points + point]
            kept = jnp.where(coarse_of == wanted, tiled[place : place + pairs, :], 0.0)
            offset = part * (chunk_points * pairs) + place
            if not isinstance(part, int):
                offset = pl.multiple_of(offset, pairs)
            target[pl.ds(offset, pairs), :] = kept.astype(jnp.bfloat16)

    parts = slot_count // chunk
    if parts == 1:
        step(0)
    else:
        lax.fori_loop(0, parts, lambda part, carry: (step(part), carry)[1], 0)


def kernel(
    kf_count, kc_count, kernel_hbm, coef_hbm, near_hbm, turned_ref, columns_ref,
    kernel_all, coef_slab, coef_cols, near, spread, factor,
    local_sem, kernel_send, kernel_recv, slab_send, slab_recv, cols_send, cols_recv,
):
    kf, kc = lax.axis_index("kf"), lax.axis_index("kc")
    group = kf_count // kc_count
    points = coef_hbm.shape[0]
    slab_points = points * kc_count
    column_points = coef_cols.shape[0] * points
    part = kf // group
    in_part = part == kc
    slot = (kf % group) * kc_count + kc

    near_copy = pltpu.make_async_copy(near_hbm, near, local_sem.at[0])
    kernel_copy = pltpu.make_async_copy(kernel_hbm, kernel_all.at[kf], local_sem.at[1])
    coef_copy = pltpu.make_async_copy(coef_hbm, coef_slab.at[kc], local_sem.at[2])
    cols_copy = pltpu.make_async_copy(coef_hbm, coef_cols.at[slot], cols_recv.at[slot])
    coef_copy.start()
    kernel_copy.start()
    near_copy.start()

    @pl.when(in_part)
    def _():
        cols_copy.start()

    barrier = pltpu.get_barrier_semaphore()
    each(1, kf_count, lambda t: signal(barrier, lax.rem(kf + t, kf_count), kc))
    each(1, kc_count, lambda t: signal(barrier, kf, lax.rem(kc + t, kc_count)))

    def greet(index):
        source_kf = kc * group + index // kc_count
        source_kc = index % kc_count

        @pl.when(jnp.logical_or(source_kf != kf, source_kc != kc))
        def _():
            signal(barrier, source_kf, source_kc)

    each(0, group * kc_count, greet)
    coef_copy.wait()
    kernel_copy.wait()
    pl.semaphore_wait(barrier, 2 * kf_count + kc_count - 2 - in_part.astype(jnp.int32))

    def slab_to(t):
        return remote(
            coef_slab.at[kc], coef_slab.at[kc], slab_send.at[t], slab_recv.at[kc],
            kf, lax.rem(kc + t, kc_count),
        )

    def cols_to(t):
        return remote(
            coef_slab.at[kc], coef_cols.at[slot], cols_send.at[t], cols_recv.at[slot],
            lax.rem(kf + t, kf_count), part,
        )

    def kernel_to(t):
        return remote(
            kernel_all.at[kf], kernel_all.at[kf], kernel_send.at[t], kernel_recv.at[kf],
            lax.rem(kf + t, kf_count), kc,
        )

    each(1, kf_count, lambda t: cols_to(t).start())

    @pl.when(jnp.logical_not(in_part))
    def _():
        cols_to(0).start()

    each(1, kc_count, lambda t: slab_to(t).start())
    each(1, kf_count, lambda t: kernel_to(t).start())
    near_copy.wait()

    def slab_from(t):
        source = lax.rem(kc + t, kc_count)
        remote(
            coef_slab.at[source], coef_slab.at[source], slab_send.at[t], slab_recv.at[source],
            kf, source,
        ).wait_recv()

    each(1, kc_count, slab_from)
    expand(coef_slab, near, kf * slab_points, spread, factor)

    def cols_from(index):
        pltpu.make_async_copy(coef_hbm, coef_cols.at[index], cols_recv.at[index]).wait()

    each(0, group * kc_count, cols_from)
    expand(coef_cols, near, kc * column_points, spread, columns_ref)

    def kernel_from(t):
        source = lax.rem(kf + t, kf_count)
        remote(
            kernel_all.at[source], kernel_all.at[source], kernel_send.at[t], kernel_recv.at[source],
            source, kc,
        ).wait_recv()

    each(1, kf_count, kernel_from)
    own_rows, width = kernel_hbm.shape
    chunk = min(kf_count, CHUNK_SLOTS)

    def rotate(index):
        rows = kernel_all[pl.ds(index * chunk, chunk)].reshape(chunk * own_rows, width)
        turned = lax.dot_general(
            factor[...], rows, (((1,), (1,)), ((), ())), preferred_element_type=jnp.float32
        )
        offset = index * (chunk * own_rows)
        if not isinstance(index, int):
            offset = pl.multiple_of(offset, chunk * own_rows)
        turned_ref[:, pl.ds(offset, chunk * own_rows)] = turned.astype(jnp.bfloat16)

    parts = kf_count // chunk
    if parts == 1:
        rotate(0)
    else:
        lax.fori_loop(0, parts, lambda index, carry: (rotate(index), carry)[1], 0)

    each(1, kf_count, lambda t: cols_to(t).wait_send())

    @pl.when(jnp.logical_not(in_part))
    def _():
        cols_to(0).wait_send()

    each(1, kc_count, lambda t: slab_to(t).wait_send())
    each(1, kf_count, lambda t: kernel_to(t).wait_send())


def shards(kf_count, kc_count, kernel_coarse, coefficients, nearest):
    own_rows, width = kernel_coarse.shape
    points, entries = coefficients.shape
    pairs = math.isqrt(entries)
    slots = kf_count // kc_count * kc_count
    slab_rows = kc_count * points * pairs
    column_rows = slots * points * pairs
    spread_rows = max(min(kc_count, CHUNK_SLOTS), min(slots, CHUNK_SLOTS)) * points * pairs
    dma = pltpu.SemaphoreType.DMA
    turned, columns = pl.pallas_call(
        functools.partial(kernel, kf_count, kc_count),
        out_shape=(
            jax.ShapeDtypeStruct((slab_rows, kf_count * own_rows), jnp.bfloat16),
            jax.ShapeDtypeStruct((column_rows, width), jnp.bfloat16),
        ),
        in_specs=[pl.BlockSpec(memory_space=pl.ANY)] * 3,
        out_specs=(pl.BlockSpec(memory_space=pltpu.VMEM), pl.BlockSpec(memory_space=pltpu.VMEM)),
        scratch_shapes=[
            pltpu.VMEM((kf_count, own_rows, width), jnp.bfloat16),
            pltpu.VMEM((kc_count, points, entries), jnp.bfloat16),
            pltpu.VMEM((slots, points, entries), jnp.bfloat16),
            pltpu.SMEM(nearest.shape, jnp.int32),
            pltpu.VMEM((spread_rows, entries), jnp.bfloat16),
            pltpu.VMEM((slab_rows, width), jnp.bfloat16),
            dma((3,)),
            dma((kf_count,)),
            dma((kf_count,)),
            dma((kc_count,)),
            dma((kc_count,)),
            dma((kf_count,)),
            dma((slots,)),
        ],
        compiler_params=pltpu.CompilerParams(collective_id=0, has_side_effects=True),
    )(kernel_coarse, coefficients, nearest)
    result = lax.dot_general(
        turned, columns, (((1,), (1,)), ((), ())), preferred_element_type=jnp.float32
    )
    return result.astype(jnp.bfloat16)


def solution(mesh):
    body = functools.partial(shards, mesh.shape["kf"], mesh.shape["kc"])
    in_specs = (P("kf", None), P(("kf", "kc"), None), P())
    return jax.shard_map(body, mesh=mesh, in_specs=in_specs, out_specs=P("kf", "kc"), check_vma=False)
```

```python
import functools
import math

import jax
import jax.numpy as jnp
from jax import lax
from jax.experimental import pallas as pl
from jax.experimental.pallas import tpu as pltpu
from jax.sharding import PartitionSpec as P

UNROLL_LIMIT = 16
CHUNK_SLOTS = 8
VMEM_ELEMENTS = 1 << 20


def each(low, high, step):
    if high - low <= UNROLL_LIMIT:
        for index in range(low, high):
            step(index)
    else:
        lax.fori_loop(low, high, lambda index, carry: (step(index), carry)[1], 0)


def remote(source, target, send_sem, recv_sem, kf, kc):
    return pltpu.make_async_remote_copy(
        src_ref=source,
        dst_ref=target,
        send_sem=send_sem,
        recv_sem=recv_sem,
        device_id={"kf": kf, "kc": kc},
        device_id_type=pl.DeviceIdType.MESH,
    )


def signal(barrier, kf, kc):
    pl.semaphore_signal(
        barrier, inc=1, device_id={"kf": kf, "kc": kc}, device_id_type=pl.DeviceIdType.MESH
    )


def expand(blocks, near, first_point, spread, target):
    slot_count, points, width = blocks.shape
    pairs = math.isqrt(width)
    column_total = target.shape[1]
    chunk = min(slot_count, CHUNK_SLOTS)
    own_block = (
        lax.broadcasted_iota(jnp.int32, (pairs, width), 1) // pairs
        == lax.broadcasted_iota(jnp.int32, (pairs, width), 0)
    )
    coarse_of = lax.broadcasted_iota(jnp.int32, (pairs, column_total), 1) // pairs
    fold = (
        lax.broadcasted_iota(jnp.int32, (width, column_total), 0) % pairs
        == lax.broadcasted_iota(jnp.int32, (width, column_total), 1) % pairs
    ).astype(jnp.bfloat16)
    chunk_points = chunk * points

    def step(part):
        for slot in range(chunk):
            block = blocks[part * chunk + slot].astype(jnp.float32)
            for point in range(points):
                row = jnp.broadcast_to(block[point : point + 1, :], (pairs, width))
                place = (slot * points + point) * pairs
                spread[place : place + pairs, :] = jnp.where(own_block, row, 0.0).astype(jnp.bfloat16)
        tiled = jnp.dot(
            spread[: chunk_points * pairs, :], fold, preferred_element_type=jnp.float32
        )
        for point in range(chunk_points):
            place = point * pairs
            wanted = near[first_point + part * chunk_points + point]
            kept = jnp.where(coarse_of == wanted, tiled[place : place + pairs, :], 0.0)
            offset = part * (chunk_points * pairs) + place
            if not isinstance(part, int):
                offset = pl.multiple_of(offset, pairs)
            target[pl.ds(offset, pairs), :] = kept.astype(jnp.bfloat16)

    parts = slot_count // chunk
    if parts == 1:
        step(0)
    else:
        lax.fori_loop(0, parts, lambda part, carry: (step(part), carry)[1], 0)


def kernel(
    kf_count, kc_count, kernel_hbm, coef_hbm, near_hbm, turned_ref, columns_ref,
    kernel_all, coef_slab, coef_cols, near, spread, factor,
    local_sem, kernel_send, kernel_recv, slab_send, slab_recv, cols_send, cols_recv,
    kernel_ready, slab_ready, cols_ready,
):
    kf, kc = lax.axis_index("kf"), lax.axis_index("kc")
    group = kf_count // kc_count
    points = coef_hbm.shape[0]
    slab_points = points * kc_count
    column_points = coef_cols.shape[0] * points
    part = kf // group
    in_part = part == kc
    slot = (kf % group) * kc_count + kc

    near_copy = pltpu.make_async_copy(near_hbm, near, local_sem.at[0])
    kernel_copy = pltpu.make_async_copy(kernel_hbm, kernel_all.at[kf], local_sem.at[1])
    coef_copy = pltpu.make_async_copy(coef_hbm, coef_slab.at[kc], local_sem.at[2])
    cols_copy = pltpu.make_async_copy(coef_hbm, coef_cols.at[slot], cols_recv.at[slot])
    coef_copy.start()
    kernel_copy.start()
    near_copy.start()

    @pl.when(in_part)
    def _():
        cols_copy.start()

    barrier = pltpu.get_barrier_semaphore()
    rank = kf * kc_count + kc
    source_count = group * kc_count
    first_source = kc * source_count

    def when(condition, step):
        pl.when(condition)(step)

    def greet_kf(p):
        when(p > kf, lambda: signal(barrier, p, kc))
        when(p * kc_count + part > rank, lambda: signal(barrier, p, part))

    def source_of(index):
        return kc * group + index // kc_count, index % kc_count

    each(0, kf_count, greet_kf)
    each(0, kc_count, lambda q: when(q > kc, lambda: signal(barrier, kf, q)))
    each(0, source_count, lambda n: when(first_source + n > rank, lambda: signal(barrier, *source_of(n))))
    lower_sources = jnp.clip(rank - first_source, 0, source_count)
    coef_copy.wait()
    kernel_copy.wait()
    greetings = 2 * kf + kc + (part < kc).astype(jnp.int32) + lower_sources
    when(greetings > 0, lambda: pl.semaphore_wait(barrier, greetings))

    each(0, kf_count, lambda p: when(p < kf, lambda: signal(kernel_ready.at[kf], p, kc)))
    each(0, source_count, lambda n: when(first_source + n < rank, lambda: signal(cols_ready.at[kf], *source_of(n))))
    each(0, kc_count, lambda q: when(q < kc, lambda: signal(slab_ready.at[kc], kf, q)))

    def slab_to(q):
        return remote(
            coef_slab.at[kc], coef_slab.at[kc], slab_send.at[q], slab_recv.at[kc], kf, q
        )

    def cols_to(p):
        return remote(
            coef_slab.at[kc], coef_cols.at[slot], cols_send.at[p], cols_recv.at[slot], p, part
        )

    def kernel_to(p):
        return remote(
            kernel_all.at[kf], kernel_all.at[kf], kernel_send.at[p], kernel_recv.at[kf], p, kc
        )

    def send_lower(p):
        when(p * kc_count + part < rank, lambda: cols_to(p).start())
        when(p < kf, lambda: kernel_to(p).start())

    def send_higher(p):
        @pl.when(p * kc_count + part > rank)
        def _():
            pl.semaphore_wait(cols_ready.at[p], 1)
            cols_to(p).start()

        @pl.when(p > kf)
        def _():
            pl.semaphore_wait(kernel_ready.at[p], 1)
            kernel_to(p).start()

    def slab_higher(q):
        @pl.when(q > kc)
        def _():
            pl.semaphore_wait(slab_ready.at[q], 1)
            slab_to(q).start()

    each(0, kf_count, send_lower)
    each(0, kc_count, lambda q: when(q < kc, lambda: slab_to(q).start()))
    each(0, kc_count, slab_higher)
    each(0, kf_count, send_higher)
    near_copy.wait()

    def slab_from(q):
        when(q != kc, lambda: remote(
            coef_slab.at[q], coef_slab.at[q], slab_send.at[q], slab_recv.at[q], kf, q
        ).wait_recv())

    each(0, kc_count, slab_from)
    expand(coef_slab, near, kf * slab_points, spread, factor)

    def cols_from(index):
        pltpu.make_async_copy(coef_hbm, coef_cols.at[index], cols_recv.at[index]).wait()

    each(0, group * kc_count, cols_from)
    expand(coef_cols, near, kc * column_points, spread, columns_ref)

    def kernel_from(p):
        when(p != kf, lambda: remote(
            kernel_all.at[p], kernel_all.at[p], kernel_send.at[p], kernel_recv.at[p], p, kc
        ).wait_recv())

    each(0, kf_count, kernel_from)
    own_rows, width = kernel_hbm.shape
    chunk = min(kf_count, CHUNK_SLOTS)

    def rotate(index):
        rows = kernel_all[pl.ds(index * chunk, chunk)].reshape(chunk * own_rows, width)
        turned = lax.dot_general(
            factor[...], rows, (((1,), (1,)), ((), ())), preferred_element_type=jnp.float32
        )
        offset = index * (chunk * own_rows)
        if not isinstance(index, int):
            offset = pl.multiple_of(offset, chunk * own_rows)
        turned_ref[:, pl.ds(offset, chunk * own_rows)] = turned.astype(jnp.bfloat16)

    parts = kf_count // chunk
    if parts == 1:
        rotate(0)
    else:
        lax.fori_loop(0, parts, lambda index, carry: (rotate(index), carry)[1], 0)

    def sent(p):
        when(p * kc_count + part != rank, lambda: cols_to(p).wait_send())
        when(p != kf, lambda: kernel_to(p).wait_send())

    each(0, kf_count, sent)
    each(0, kc_count, lambda q: when(q != kc, lambda: slab_to(q).wait_send()))


def shards(kf_count, kc_count, kernel_coarse, coefficients, nearest):
    own_rows, width = kernel_coarse.shape
    points, entries = coefficients.shape
    pairs = math.isqrt(entries)
    slots = kf_count // kc_count * kc_count
    slab_rows = kc_count * points * pairs
    column_rows = slots * points * pairs
    spread_rows = max(min(kc_count, CHUNK_SLOTS), min(slots, CHUNK_SLOTS)) * points * pairs
    dma, regular = pltpu.SemaphoreType.DMA, pltpu.SemaphoreType.REGULAR
    fits = (slab_rows + column_rows) * width <= VMEM_ELEMENTS
    place = pltpu.VMEM if fits else jax.ShapeDtypeStruct
    turned, columns = pl.pallas_call(
        functools.partial(kernel, kf_count, kc_count),
        out_shape=(
            place((slab_rows, kf_count * own_rows), jnp.bfloat16),
            place((column_rows, width), jnp.bfloat16),
        ),
        in_specs=[pl.BlockSpec(memory_space=pl.ANY)] * 3,
        out_specs=(pl.BlockSpec(memory_space=pltpu.VMEM), pl.BlockSpec(memory_space=pltpu.VMEM)),
        scratch_shapes=[
            pltpu.VMEM((kf_count, own_rows, width), jnp.bfloat16),
            pltpu.VMEM((kc_count, points, entries), jnp.bfloat16),
            pltpu.VMEM((slots, points, entries), jnp.bfloat16),
            pltpu.SMEM(nearest.shape, jnp.int32),
            pltpu.VMEM((spread_rows, entries), jnp.bfloat16),
            pltpu.VMEM((slab_rows, width), jnp.bfloat16),
            dma((3,)),
            dma((kf_count,)),
            dma((kf_count,)),
            dma((kc_count,)),
            dma((kc_count,)),
            dma((kf_count,)),
            dma((slots,)),
            regular((kf_count,)),
            regular((kc_count,)),
            regular((kf_count,)),
        ],
        compiler_params=pltpu.CompilerParams(collective_id=0, has_side_effects=True),
    )(kernel_coarse, coefficients, nearest)
    result = lax.dot_general(
        turned, columns, (((1,), (1,)), ((), ())), preferred_element_type=jnp.float32
    )
    return result.astype(jnp.bfloat16)


def solution(mesh):
    body = functools.partial(shards, mesh.shape["kf"], mesh.shape["kc"])
    in_specs = (P("kf", None), P(("kf", "kc"), None), P())
    return jax.shard_map(body, mesh=mesh, in_specs=in_specs, out_specs=P("kf", "kc"), check_vma=False)
```

```python
import functools
import math

import jax
import jax.numpy as jnp
from jax import lax
from jax.experimental import pallas as pl
from jax.experimental.pallas import tpu as pltpu
from jax.sharding import PartitionSpec as P

UNROLL_LIMIT = 16
CHUNK_SLOTS = 8
VMEM_ELEMENTS = 1 << 20


def each(low, high, step):
    if high - low <= UNROLL_LIMIT:
        for index in range(low, high):
            step(index)
    else:
        lax.fori_loop(low, high, lambda index, carry: (step(index), carry)[1], 0)


def remote(source, target, send_sem, recv_sem, kf, kc):
    return pltpu.make_async_remote_copy(
        src_ref=source,
        dst_ref=target,
        send_sem=send_sem,
        recv_sem=recv_sem,
        device_id={"kf": kf, "kc": kc},
        device_id_type=pl.DeviceIdType.MESH,
    )


def signal(barrier, kf, kc):
    pl.semaphore_signal(
        barrier, inc=1, device_id={"kf": kf, "kc": kc}, device_id_type=pl.DeviceIdType.MESH
    )


def expand(blocks, near, first_point, spread, fold, target):
    slot_count, points, width = blocks.shape
    pairs = math.isqrt(width)
    column_total = target.shape[1]
    chunk = min(slot_count, CHUNK_SLOTS)
    own_block = (
        lax.broadcasted_iota(jnp.int32, (pairs, width), 1) // pairs
        == lax.broadcasted_iota(jnp.int32, (pairs, width), 0)
    )
    coarse_of = lax.broadcasted_iota(jnp.int32, (pairs, column_total), 1) // pairs
    chunk_points = chunk * points

    def step(part):
        for slot in range(chunk):
            block = blocks[part * chunk + slot].astype(jnp.float32)
            for point in range(points):
                row = jnp.broadcast_to(block[point : point + 1, :], (pairs, width))
                place = (slot * points + point) * pairs
                spread[place : place + pairs, :] = jnp.where(own_block, row, 0.0).astype(jnp.bfloat16)
        tiled = jnp.dot(
            spread[: chunk_points * pairs, :], fold[...], preferred_element_type=jnp.float32
        )
        for point in range(chunk_points):
            place = point * pairs
            wanted = near[first_point + part * chunk_points + point]
            kept = jnp.where(coarse_of == wanted, tiled[place : place + pairs, :], 0.0)
            offset = part * (chunk_points * pairs) + place
            if not isinstance(part, int):
                offset = pl.multiple_of(offset, pairs)
            target[pl.ds(offset, pairs), :] = kept.astype(jnp.bfloat16)

    parts = slot_count // chunk
    if parts == 1:
        step(0)
    else:
        lax.fori_loop(0, parts, lambda part, carry: (step(part), carry)[1], 0)


def kernel(
    kf_count, kc_count, kernel_hbm, coef_hbm, near_hbm, turned_ref, columns_ref,
    kernel_all, coef_slab, coef_cols, near, spread, fold, factor,
    local_sem, kernel_send, kernel_recv, slab_send, slab_recv, cols_send, cols_recv,
    kernel_ready, slab_ready, cols_ready,
):
    kf, kc = lax.axis_index("kf"), lax.axis_index("kc")
    group = kf_count // kc_count
    points = coef_hbm.shape[0]
    slab_points = points * kc_count
    column_points = coef_cols.shape[0] * points
    part = kf // group
    in_part = part == kc
    slot = (kf % group) * kc_count + kc

    near_copy = pltpu.make_async_copy(near_hbm, near, local_sem.at[0])
    kernel_copy = pltpu.make_async_copy(kernel_hbm, kernel_all.at[kf], local_sem.at[1])
    coef_copy = pltpu.make_async_copy(coef_hbm, coef_slab.at[kc], local_sem.at[2])
    cols_copy = pltpu.make_async_copy(coef_hbm, coef_cols.at[slot], cols_recv.at[slot])
    coef_copy.start()
    kernel_copy.start()
    near_copy.start()

    @pl.when(in_part)
    def _():
        cols_copy.start()

    barrier = pltpu.get_barrier_semaphore()
    rank = kf * kc_count + kc
    source_count = group * kc_count
    first_source = kc * source_count

    def when(condition, step):
        pl.when(condition)(step)

    def greet_kf(p):
        when(p > kf, lambda: signal(barrier, p, kc))
        when(p * kc_count + part > rank, lambda: signal(barrier, p, part))

    def source_of(index):
        return kc * group + index // kc_count, index % kc_count

    each(0, kf_count, greet_kf)
    each(0, kc_count, lambda q: when(q > kc, lambda: signal(barrier, kf, q)))
    each(0, source_count, lambda n: when(first_source + n > rank, lambda: signal(barrier, *source_of(n))))
    lower_sources = jnp.clip(rank - first_source, 0, source_count)
    pairs = math.isqrt(coef_hbm.shape[1])
    fold[...] = (
        lax.broadcasted_iota(jnp.int32, fold.shape, 0) % pairs
        == lax.broadcasted_iota(jnp.int32, fold.shape, 1) % pairs
    ).astype(jnp.bfloat16)
    coef_copy.wait()
    kernel_copy.wait()
    greetings = 2 * kf + kc + (part < kc).astype(jnp.int32) + lower_sources
    when(greetings > 0, lambda: pl.semaphore_wait(barrier, greetings))

    each(0, kf_count, lambda p: when(p < kf, lambda: signal(kernel_ready.at[kf], p, kc)))
    each(0, source_count, lambda n: when(first_source + n < rank, lambda: signal(cols_ready.at[kf], *source_of(n))))
    each(0, kc_count, lambda q: when(q < kc, lambda: signal(slab_ready.at[kc], kf, q)))

    def slab_to(q):
        return remote(
            coef_slab.at[kc], coef_slab.at[kc], slab_send.at[q], slab_recv.at[kc], kf, q
        )

    def cols_to(p):
        return remote(
            coef_slab.at[kc], coef_cols.at[slot], cols_send.at[p], cols_recv.at[slot], p, part
        )

    def kernel_to(p):
        return remote(
            kernel_all.at[kf], kernel_all.at[kf], kernel_send.at[p], kernel_recv.at[kf], p, kc
        )

    def send_lower(p):
        when(p * kc_count + part < rank, lambda: cols_to(p).start())
        when(p < kf, lambda: kernel_to(p).start())

    def send_higher(p):
        @pl.when(p * kc_count + part > rank)
        def _():
            pl.semaphore_wait(cols_ready.at[p], 1)
            cols_to(p).start()

        @pl.when(p > kf)
        def _():
            pl.semaphore_wait(kernel_ready.at[p], 1)
            kernel_to(p).start()

    def slab_higher(q):
        @pl.when(q > kc)
        def _():
            pl.semaphore_wait(slab_ready.at[q], 1)
            slab_to(q).start()

    each(0, kf_count, send_lower)
    each(0, kc_count, lambda q: when(q < kc, lambda: slab_to(q).start()))
    each(0, kc_count, slab_higher)
    each(0, kf_count, send_higher)
    near_copy.wait()

    def slab_from(q):
        when(q != kc, lambda: remote(
            coef_slab.at[q], coef_slab.at[q], slab_send.at[q], slab_recv.at[q], kf, q
        ).wait_recv())

    each(0, kc_count, slab_from)
    expand(coef_slab, near, kf * slab_points, spread, fold, factor)

    def cols_from(index):
        pltpu.make_async_copy(coef_hbm, coef_cols.at[index], cols_recv.at[index]).wait()

    each(0, group * kc_count, cols_from)
    expand(coef_cols, near, kc * column_points, spread, fold, columns_ref)

    def kernel_from(p):
        when(p != kf, lambda: remote(
            kernel_all.at[p], kernel_all.at[p], kernel_send.at[p], kernel_recv.at[p], p, kc
        ).wait_recv())

    each(0, kf_count, kernel_from)
    own_rows, width = kernel_hbm.shape
    chunk = min(kf_count, CHUNK_SLOTS)

    def rotate(index):
        rows = kernel_all[pl.ds(index * chunk, chunk)].reshape(chunk * own_rows, width)
        turned = lax.dot_general(
            factor[...], rows, (((1,), (1,)), ((), ())), preferred_element_type=jnp.float32
        )
        offset = index * (chunk * own_rows)
        if not isinstance(index, int):
            offset = pl.multiple_of(offset, chunk * own_rows)
        turned_ref[:, pl.ds(offset, chunk * own_rows)] = turned.astype(jnp.bfloat16)

    parts = kf_count // chunk
    if parts == 1:
        rotate(0)
    else:
        lax.fori_loop(0, parts, lambda index, carry: (rotate(index), carry)[1], 0)

    def sent(p):
        when(p * kc_count + part != rank, lambda: cols_to(p).wait_send())
        when(p != kf, lambda: kernel_to(p).wait_send())

    each(0, kf_count, sent)
    each(0, kc_count, lambda q: when(q != kc, lambda: slab_to(q).wait_send()))


def shards(kf_count, kc_count, kernel_coarse, coefficients, nearest):
    own_rows, width = kernel_coarse.shape
    points, entries = coefficients.shape
    pairs = math.isqrt(entries)
    slots = kf_count // kc_count * kc_count
    slab_rows = kc_count * points * pairs
    column_rows = slots * points * pairs
    spread_rows = max(min(kc_count, CHUNK_SLOTS), min(slots, CHUNK_SLOTS)) * points * pairs
    dma, regular = pltpu.SemaphoreType.DMA, pltpu.SemaphoreType.REGULAR
    fits = (slab_rows + column_rows) * width <= VMEM_ELEMENTS
    place = pltpu.VMEM if fits else jax.ShapeDtypeStruct
    turned, columns = pl.pallas_call(
        functools.partial(kernel, kf_count, kc_count),
        out_shape=(
            place((slab_rows, kf_count * own_rows), jnp.bfloat16),
            place((column_rows, width), jnp.bfloat16),
        ),
        in_specs=[pl.BlockSpec(memory_space=pl.ANY)] * 3,
        out_specs=(pl.BlockSpec(memory_space=pltpu.VMEM), pl.BlockSpec(memory_space=pltpu.VMEM)),
        scratch_shapes=[
            pltpu.VMEM((kf_count, own_rows, width), jnp.bfloat16),
            pltpu.VMEM((kc_count, points, entries), jnp.bfloat16),
            pltpu.VMEM((slots, points, entries), jnp.bfloat16),
            pltpu.SMEM(nearest.shape, jnp.int32),
            pltpu.VMEM((spread_rows, entries), jnp.bfloat16),
            pltpu.VMEM((entries, width), jnp.bfloat16),
            pltpu.VMEM((slab_rows, width), jnp.bfloat16),
            dma((3,)),
            dma((kf_count,)),
            dma((kf_count,)),
            dma((kc_count,)),
            dma((kc_count,)),
            dma((kf_count,)),
            dma((slots,)),
            regular((kf_count,)),
            regular((kc_count,)),
            regular((kf_count,)),
        ],
        compiler_params=pltpu.CompilerParams(collective_id=0, has_side_effects=True),
    )(kernel_coarse, coefficients, nearest)
    result = lax.dot_general(
        turned, columns, (((1,), (1,)), ((), ())), preferred_element_type=jnp.float32
    )
    return result.astype(jnp.bfloat16)


def solution(mesh):
    body = functools.partial(shards, mesh.shape["kf"], mesh.shape["kc"])
    in_specs = (P("kf", None), P(("kf", "kc"), None), P())
    return jax.shard_map(body, mesh=mesh, in_specs=in_specs, out_specs=P("kf", "kc"), check_vma=False)
```
